32 devices in a mesh: batch: 2 (over x), seq: 16 (over z, y, core).
Axes of the slice: x: 2, y: 2, z: 4, core: 2. Of those that a mesh axis runs over, the one named last changes fastest.
Arguments:
- inputs: bfloat16 [8, 2048, 1152], P('batch', 'seq'), may hold values from -6 to 6
- input_gain: bfloat16 [1152], P(('batch', 'seq')), may hold values from 0.25 to 1.75
- query_weight: bfloat16 [1152, 1024], P(('batch', 'seq')), may hold values from -0.1875 to 0.1875
- key_weight: bfloat16 [1152, 256], P(('batch', 'seq')), may hold values from -0.1875 to 0.1875
- value_weight: bfloat16 [1152, 256], P(('batch', 'seq')), may hold values from -0.1875 to 0.1875
- query_norm: bfloat16 [256], P(('batch', 'seq')), may hold values from 0.25 to 1.75
- key_norm: bfloat16 [256], P(('batch', 'seq')), may hold values from 0.25 to 1.75
- output_weight: bfloat16 [1024, 1152], P(('batch', 'seq')), may hold values from -0.1875 to 0.1875
- attention_gain: bfloat16 [1152], P(('batch', 'seq')), may hold values from 0.25 to 1.75
- feedforward_gain: bfloat16 [1152], P(('batch', 'seq')), may hold values from 0.25 to 1.75
- gate_weight: bfloat16 [1152, 6912], P(('batch', 'seq')), may hold values from -0.1875 to 0.1875
- up_weight: bfloat16 [1152, 6912], P(('batch', 'seq')), may hold values from -0.1875 to 0.1875
- down_weight: bfloat16 [6912, 1152], P(('batch', 'seq')), may hold values from -0.078125 to 0.078125
- closing_gain: bfloat16 [1152], P(('batch', 'seq')), may hold values from 0.25 to 1.75
- cotangent: bfloat16 [8, 2048, 1152], P('batch', 'seq'), may hold values from -6 to 6
Outputs:
- layer_out: bfloat16 [8, 2048, 1152], P('batch', 'seq')
- input_grad: bfloat16 [8, 2048, 1152], P('batch', 'seq')
- input_gain_grad: float32 [1152], P(('batch', 'seq'))
- query_weight_grad: float32 [1152, 1024], P(('batch', 'seq'))
- key_weight_grad: float32 [1152, 256], P(('batch', 'seq'))
- value_weight_grad: float32 [1152, 256], P(('batch', 'seq'))
- query_norm_grad: float32 [256], P(('batch', 'seq'))
- key_norm_grad: float32 [256], P(('batch', 'seq'))
- output_weight_grad: float32 [1024, 1152], P(('batch', 'seq'))
- attention_gain_grad: float32 [1152], P(('batch', 'seq'))
- feedforward_gain_grad: float32 [1152], P(('batch', 'seq'))
- gate_weight_grad: float32 [1152, 6912], P(('batch', 'seq'))
- up_weight_grad: float32 [1152, 6912], P(('batch', 'seq'))
- down_weight_grad: float32 [6912, 1152], P(('batch', 'seq'))
- closing_gain_grad: float32 [1152], P(('batch', 'seq'))
The draws below stay inside these ranges and needn't reach their ends.
All inputs are finite; a program needn't handle non-finite values.
Results may differ from the reference program's by a relative error of at most 0.035.
Values may be sent and summed in bfloat16 or wider, within the bound.
No kernel may reach another device: no remote copies, remote signals or barrier semaphores. Data moves between devices by JAX's collectives and lax.ppermute only.
A program may use at most 384 MiB of HBM per device.

```python
import math
import jax
import jax.numpy as jnp
from jax import lax

D = 1152
H = 4
HD = 256
FF = 6912
SEQS = 8
LEN = 2048


def block_levels(stream_key, shape, split, least, high):
    level, own = 1.0, jax.random.fold_in(stream_key, 6)
    for axis_at, shards_of in split:
        heights = jnp.exp(jax.random.uniform(jax.random.fold_in(own, axis_at), (shards_of,), jnp.float32, least / len(split), high / len(split)))
        level = level * jnp.repeat(heights, shape[axis_at] // shards_of).reshape([-1 if axis == axis_at else 1 for axis in range(len(shape))])
    return level


def scatter_about(own_key, shape, spread, reach, pieces=(), kind=jnp.bfloat16):
    entries = jax.random.normal(own_key, shape, jnp.float32) * spread
    if len(pieces) > 0:
        entries = block_levels(own_key, shape, pieces, -0.22, 0.18) * entries
    return jnp.clip(entries, min=-reach, max=reach).astype(kind)


def setup_inputs(seed: int = 0) -> dict:
    splits = jax.random.split(jax.random.key(seed), 16)
    inputs = scatter_about(splits[0], (SEQS, LEN, D), 1.0, 6.0, ((0, 2), (1, 16)))
    input_gain = jnp.clip(1.0 + 0.15 * jax.random.normal(splits[1], (D,), jnp.float32), 0.25, 1.75).astype(jnp.bfloat16)
    query_weight = scatter_about(splits[2], (D, H * HD), D ** -0.5, 0.1875, ((0, 32),))
    key_weight = scatter_about(splits[3], (D, HD), D ** -0.5, 0.1875, ((0, 32),))
    value_weight = scatter_about(splits[4], (D, HD), D ** -0.5, 0.1875, ((0, 32),))
    query_norm = jnp.clip(1.0 + 0.15 * jax.random.normal(splits[5], (HD,), jnp.float32), 0.25, 1.75).astype(jnp.bfloat16)
    key_norm = jnp.clip(1.0 + 0.15 * jax.random.normal(splits[6], (HD,), jnp.float32), 0.25, 1.75).astype(jnp.bfloat16)
    output_weight = scatter_about(splits[7], (H * HD, D), (H * HD) ** -0.5, 0.1875, ((0, 32),))
    attention_gain = jnp.clip(1.0 + 0.15 * jax.random.normal(splits[8], (D,), jnp.float32), 0.25, 1.75).astype(jnp.bfloat16)
    feedforward_gain = jnp.clip(1.0 + 0.15 * jax.random.normal(splits[9], (D,), jnp.float32), 0.25, 1.75).astype(jnp.bfloat16)
    gate_weight = scatter_about(splits[10], (D, FF), D ** -0.5, 0.1875, ((0, 32),))
    up_weight = scatter_about(splits[11], (D, FF), D ** -0.5, 0.1875, ((0, 32),))
    down_weight = scatter_about(splits[12], (FF, D), FF ** -0.5, 0.078125, ((0, 32),))
    closing_gain = jnp.clip(1.0 + 0.15 * jax.random.normal(splits[13], (D,), jnp.float32), 0.25, 1.75).astype(jnp.bfloat16)
    cotangent = scatter_about(splits[14], (SEQS, LEN, D), 1.0, 6.0, ((0, 2), (1, 16)))
    return {"inputs": inputs, "input_gain": input_gain, "query_weight": query_weight, "key_weight": key_weight, "value_weight": value_weight, "query_norm": query_norm, "key_norm": key_norm, "output_weight": output_weight, "attention_gain": attention_gain, "feedforward_gain": feedforward_gain, "gate_weight": gate_weight, "up_weight": up_weight, "down_weight": down_weight, "closing_gain": closing_gain, "cotangent": cotangent}


@jax.custom_vjp
def low(v):
    return lax.optimization_barrier(v.astype(jnp.bfloat16)).astype(jnp.float32)

@jax.custom_vjp
def low_back(v):
    return v

def low_keep(v):
    return (low(v), None)

def low_pass(kept, grad):
    return (grad,)

def back_keep(v):
    return (v, None)

def back_low(kept, grad):
    return (low(grad),)
low.defvjp(low_keep, low_pass)
low_back.defvjp(back_keep, back_low)
epsilon = 1e-06
rope_base = 1000000.0
gelu_coef = 0.7978845608028654
masked_value = -1e+30

def normed(vector, gain_vec):
    return vector * lax.rsqrt(lax.optimization_barrier(jnp.mean(vector * vector, axis=-1, keepdims=True)) + epsilon) * gain_vec

def gelu_tanh(vector):
    inner_arg = gelu_coef * (vector + 0.044715 * vector * vector * vector)
    return 0.5 * vector * (1.0 + jnp.tanh(inner_arg))

def angles(positions, head_width):
    half_dim = head_width // 2
    inv_freq = jnp.exp(jnp.arange(half_dim, dtype=jnp.float32) * (-2.0 * math.log(rope_base) / head_width))
    turned = positions.astype(jnp.float32)[:, None] * inv_freq[None, :]
    return (jnp.cos(turned), jnp.sin(turned))

def rotate(vector, cos_vals, sine_vals):
    half_dim = vector.shape[-1] // 2
    lower_half = vector[..., :half_dim]
    upper_half = vector[..., half_dim:]
    return jnp.concatenate([lower_half * cos_vals - upper_half * sine_vals, upper_half * cos_vals + lower_half * sine_vals], axis=-1)

def matmul(left_mat, right_mat):
    return jnp.dot(left_mat, right_mat, precision=lax.Precision.HIGHEST, preferred_element_type=jnp.float32)

def layer(seq_in, input_gain, query_weight, key_weight, value_weight, query_norm, key_norm, output_weight, attention_gain, feedforward_gain, gate_weight, up_weight, down_weight, closing_gain):
    seq_len = seq_in.shape[0]
    positions = jnp.arange(seq_len, dtype=jnp.int32)
    cos_vals, sine_vals = angles(positions, HD)
    normed_in = low(normed(seq_in, input_gain))
    query_raw = low_back(matmul(normed_in, query_weight)).reshape(seq_len, H, HD)
    key_raw = low_back(matmul(normed_in, key_weight))
    value_rows = low(low_back(matmul(normed_in, value_weight)))
    query_rot = low(rotate(normed(query_raw, query_norm), cos_vals[:, None, :], sine_vals[:, None, :]))
    key_rot = low(rotate(normed(key_raw, key_norm), cos_vals, sine_vals))
    block_rows = math.gcd(seq_len, 512)
    score_scale = HD ** (-0.5)

    def attend(block_index):
        offset = block_index * block_rows
        query_block = lax.dynamic_slice_in_dim(query_rot, offset, block_rows, 0)
        scores = low_back(jnp.einsum('qhd,kd->hqk', query_block, key_rot, precision=lax.Precision.HIGHEST) * score_scale)
        query_pos = offset + jnp.arange(block_rows, dtype=jnp.int32)
        allowed = query_pos[:, None] >= positions[None, :]
        masked = jnp.where(allowed[None], scores, masked_value)
        prob_vals = low(jax.nn.softmax(masked, axis=-1))
        return jnp.einsum('hqk,kd->qhd', prob_vals, value_rows, precision=lax.Precision.HIGHEST)
    blocks = lax.map(jax.checkpoint(attend), jnp.arange(seq_len // block_rows, dtype=jnp.int32))
    attn_rows = low(low_back(blocks.reshape(seq_len, H * HD)))
    attn_proj = low_back(matmul(attn_rows, output_weight))
    resid = seq_in + normed(attn_proj, attention_gain)
    normed_mid = low(normed(resid, feedforward_gain))
    gate_vals = low_back(matmul(normed_mid, gate_weight))
    up_vals = low_back(matmul(normed_mid, up_weight))
    hidden = low(gelu_tanh(gate_vals) * up_vals)
    down_vals = low_back(matmul(hidden, down_weight))
    return resid + normed(down_vals, closing_gain)

def reference(inputs, input_gain, query_weight, key_weight, value_weight, query_norm, key_norm, output_weight, attention_gain, feedforward_gain, gate_weight, up_weight, down_weight, closing_gain, cotangent):
    weight_list = tuple((weight_item.astype(jnp.float32) for weight_item in (input_gain, query_weight, key_weight, value_weight, query_norm, key_norm, output_weight, attention_gain, feedforward_gain, gate_weight, up_weight, down_weight, closing_gain)))

    def one_sequence(totals, paired):
        seq_in, seq_cot = paired
        result, pullback = jax.vjp(layer, seq_in.astype(jnp.float32), *weight_list)
        gradients = pullback(seq_cot.astype(jnp.float32))
        totals = tuple((total_item + grad_item for total_item, grad_item in zip(totals, gradients[1:])))
        return (totals, (result.astype(jnp.bfloat16), gradients[0].astype(jnp.bfloat16)))
    zero_sums = tuple((jnp.zeros(weight_item.shape, jnp.float32) for weight_item in weight_list))
    totals, (outputs, input_grads) = lax.scan(one_sequence, zero_sums, (inputs, cotangent))
    return (outputs, input_grads, totals[0], totals[1], totals[2], totals[3], totals[4], totals[5], totals[6], totals[7], totals[8], totals[9], totals[10], totals[11], totals[12])
```

```python
import math

import jax
import jax.numpy as jnp
from jax import lax
from jax.experimental import pallas as pl
from jax.experimental.pallas import tpu as pltpu
from jax.sharding import Mesh
from jax.sharding import PartitionSpec as P

H = 4
HD = 256

epsilon = 1e-06
rope_base = 1000000.0
gelu_coef = 0.7978845608028654
masked_value = -1e30


f32 = jnp.float32
bf16 = jnp.bfloat16


def normed(vector, gain_vec):
    return (
        vector * lax.rsqrt(jnp.mean(vector * vector, axis=-1, keepdims=True) + epsilon) * gain_vec
    )


def gelu_tanh(vector):
    inner_arg = gelu_coef * (vector + 0.044715 * vector * vector * vector)
    return 0.5 * vector * (1.0 + jnp.tanh(inner_arg))


def gated(gate_in, up_in):
    return gelu_tanh(gate_in) * up_in


def angles(positions, head_width):
    half_dim = head_width // 2
    inv_freq = jnp.exp(
        jnp.arange(half_dim, dtype=jnp.float32) * (-2.0 * math.log(rope_base) / head_width)
    )
    turned = positions.astype(jnp.float32)[:, None] * inv_freq[None, :]
    return (jnp.cos(turned), jnp.sin(turned))


def rotate(vector, cos_vals, sine_vals):
    half_dim = vector.shape[-1] // 2
    lower_half = vector[..., :half_dim]
    upper_half = vector[..., half_dim:]
    return jnp.concatenate(
        [
            lower_half * cos_vals - upper_half * sine_vals,
            upper_half * cos_vals + lower_half * sine_vals,
        ],
        axis=-1,
    )


def matmul(left_mat, right_mat):
    return jnp.dot(left_mat, right_mat, preferred_element_type=f32)


def inner_rows(left_mat, right_mat):
    return lax.dot_general(
        left_mat, right_mat, (((0,), (0,)), ((), ())), preferred_element_type=f32
    )


def times_trans(left_mat, right_mat):
    return lax.dot_general(
        left_mat, right_mat, (((1,), (1,)), ((), ())), preferred_element_type=f32
    )


def hop(value, axis, shift=1):
    size = lax.axis_size(axis)
    return lax.ppermute(value, axis, [(i, (i + shift) % size) for i in range(size)])


def pick(value, index, axis=0):
    return lax.dynamic_index_in_dim(value, index, axis, keepdims=False)


def ordered(first_is_own, own, other, axis):
    return jnp.stack(
        [jnp.where(first_is_own, own, other), jnp.where(first_is_own, other, own)], axis
    )


def gather_plane(piece):
    size = lax.axis_size("r")
    rank, side = lax.axis_index("r"), lax.axis_index("batch")
    near = [piece] + [hop(piece, "r", k) for k in range(1, size)]
    far = [hop(p, "batch") for p in near]
    whole = jnp.zeros((2 * size,) + piece.shape, piece.dtype)
    for k in range(size):
        slot = lax.rem(rank - k + size, size)
        whole = lax.dynamic_update_index_in_dim(whole, near[k], side * size + slot, 0)
        whole = lax.dynamic_update_index_in_dim(whole, far[k], (1 - side) * size + slot, 0)
    return whole


def scatter_plane(whole):
    size = lax.axis_size("r")
    rank, side = lax.axis_index("r"), lax.axis_index("batch")
    whole = whole.reshape((2, size) + whole.shape[1:])
    mine, yours = pick(whole, side), pick(whole, 1 - side)
    total = None
    for k in range(size - 1, -1, -1):
        slot = lax.rem(rank + k, size)
        got = hop(pick(yours, slot), "batch")
        here = pick(mine, slot).astype(f32) + got.astype(f32)
        if k > 0:
            here = hop(here.astype(bf16), "r", k).astype(f32)
        total = here if total is None else total + here
    return total


def gather_chips(piece):
    size = lax.axis_size("r")
    rank, side, row = lax.axis_index("r"), lax.axis_index("batch"), lax.axis_index("t")
    line = jnp.zeros((size,) + piece.shape, piece.dtype)
    for k in range(size):
        got = piece if k == 0 else hop(piece, "r", k)
        line = lax.dynamic_update_index_in_dim(line, got, lax.rem(rank - k + size, size), 0)
    line_b, line_t = hop(line, "batch"), hop(line, "t")
    line_bt = hop(line_b, "t")
    whole = jnp.zeros((2, size, 2) + piece.shape, piece.dtype)
    rest = (0,) * piece.ndim
    for value, b, t in (
        (line, side, row),
        (line_b, 1 - side, row),
        (line_t, side, 1 - row),
        (line_bt, 1 - side, 1 - row),
    ):
        whole = lax.dynamic_update_slice(whole, value[None, :, None], (b, 0, t) + rest)
    return whole.reshape((4 * size,) + piece.shape)


def scatter_chips(whole):
    size = lax.axis_size("r")
    rank, side, row = lax.axis_index("r"), lax.axis_index("batch"), lax.axis_index("t")
    whole = whole.reshape((2, size, 2) + whole.shape[1:])
    part = pick(whole, row, 2).astype(f32) + hop(pick(whole, 1 - row, 2), "t").astype(f32)
    part = part.astype(bf16)
    part = pick(part, side).astype(f32) + hop(pick(part, 1 - side), "batch").astype(f32)
    part = part.astype(bf16)
    total = pick(part, rank).astype(f32)
    for k in range(1, size):
        total = total + hop(pick(part, lax.rem(rank + k, size)), "r", k).astype(f32)
    return total


def heads_down(value):
    return jnp.concatenate([value[:, h * HD : (h + 1) * HD] for h in range(H)], axis=0)


def key_chunk(length):
    return math.gcd(length, 512)


def flash_forward(q_ref, k_ref, v_ref, qpos_ref, kpos_ref, o_ref, lse_ref, acc_ref, m_ref, l_ref):
    queries = heads_down(q_ref[0])
    rows = queries.shape[0]
    length = k_ref.shape[2]
    chunk = key_chunk(length)
    qpos = jnp.concatenate([qpos_ref[...]] * H, axis=0)
    acc_ref[...] = jnp.zeros_like(acc_ref)
    m_ref[...] = jnp.full_like(m_ref, masked_value)
    l_ref[...] = jnp.zeros_like(l_ref)

    def step(i, carry):
        start = pl.multiple_of(i * chunk, chunk)
        keys = k_ref[0, 0, pl.ds(start, chunk), :]
        vals = v_ref[0, 0, pl.ds(start, chunk), :]
        scores = times_trans(queries, keys) * (HD**-0.5)
        allowed = qpos[:, :1] >= kpos_ref[:, pl.ds(start, chunk)]
        scores = jnp.where(allowed, scores, masked_value)
        old = m_ref[:, :1]
        new = jnp.maximum(old, jnp.max(scores, axis=-1, keepdims=True))
        weights = jnp.where(allowed, jnp.exp(scores - new), 0.0)
        factor = jnp.exp(old - new)
        l_ref[...] = jnp.broadcast_to(
            l_ref[:, :1] * factor + jnp.sum(weights, axis=-1, keepdims=True), l_ref.shape
        )
        m_ref[...] = jnp.broadcast_to(new, m_ref.shape)
        acc_ref[...] = acc_ref[...] * factor + matmul(weights.astype(bf16), vals)
        return carry

    lax.fori_loop(0, length // chunk, step, 0)
    out = acc_ref[...] / l_ref[:, :1]
    share = rows // H
    for h in range(H):
        o_ref[0, :, h * HD : (h + 1) * HD] = out[h * share : (h + 1) * share]
    lse_ref[0] = m_ref[...] + jnp.log(l_ref[...])


def flash_backward(
    q_ref, do_ref, o_ref, lse_ref, k_ref, v_ref, qpos_ref, kpos_ref, dq_ref, dkv_ref, acc_ref
):
    queries = heads_down(q_ref[0])
    douts = heads_down(do_ref[0])
    outs = heads_down(o_ref[0])
    delta = jnp.sum(douts.astype(f32) * outs, axis=-1, keepdims=True)
    lse = lse_ref[0][:, :1]
    rows = queries.shape[0]
    length = k_ref.shape[2]
    chunk = key_chunk(length)
    qpos = jnp.concatenate([qpos_ref[...]] * H, axis=0)
    acc_ref[...] = jnp.zeros_like(acc_ref)
    scale = HD**-0.5

    def step(i, carry):
        start = pl.multiple_of(i * chunk, chunk)
        keys = k_ref[0, 0, pl.ds(start, chunk), :]
        vals = v_ref[0, 0, pl.ds(start, chunk), :]
        scores = times_trans(queries, keys) * scale
        allowed = qpos[:, :1] >= kpos_ref[:, pl.ds(start, chunk)]
        probs = jnp.where(allowed, jnp.exp(scores - lse), 0.0)
        dprobs = times_trans(douts, vals)
        dscores = (probs * (dprobs - delta)).astype(bf16)
        acc_ref[...] += matmul(dscores, keys)
        dkv_ref[0, 0, pl.ds(start, chunk), :] = (inner_rows(dscores, queries) * scale).astype(bf16)
        dkv_ref[1, 0, pl.ds(start, chunk), :] = inner_rows(probs.astype(bf16), douts).astype(bf16)
        return carry

    lax.fori_loop(0, length // chunk, step, 0)
    out = acc_ref[...] * scale
    share = rows // H
    for h in range(H):
        dq_ref[0, :, h * HD : (h + 1) * HD] = out[h * share : (h + 1) * share]


def attend(queries, keys_values, qpos, kpos, first):
    _, local, wide = queries.shape
    _, count, length, _ = keys_values.shape
    rows = H * local
    row_spec = pl.BlockSpec((1, local, wide), lambda s: (s + first, 0, 0))
    return pl.pallas_call(
        flash_forward,
        grid=(count,),
        in_specs=[
            row_spec,
            pl.BlockSpec((1, 1, length, HD), lambda s: (0, s, 0, 0)),
            pl.BlockSpec((1, 1, length, HD), lambda s: (1, s, 0, 0)),
            pl.BlockSpec((local, 128), lambda s: (0, 0)),
            pl.BlockSpec((1, length), lambda s: (0, 0)),
        ],
        out_specs=[
            pl.BlockSpec((1, local, wide), lambda s: (s, 0, 0)),
            pl.BlockSpec((1, rows, 128), lambda s: (s, 0, 0)),
        ],
        out_shape=[
            jax.ShapeDtypeStruct((count, local, wide), f32),
            jax.ShapeDtypeStruct((count, rows, 128), f32),
        ],
        scratch_shapes=[
            pltpu.VMEM((rows, HD), f32),
            pltpu.VMEM((rows, 128), f32),
            pltpu.VMEM((rows, 128), f32),
        ],
        cost_estimate=pl.CostEstimate(
            flops=4 * count * rows * length * HD,
            bytes_accessed=count * (4 * length * HD + 6 * rows * HD),
            transcendentals=count * rows * length,
        ),
        name="attend",
    )(queries, keys_values, keys_values, qpos, kpos)


def attend_back(queries, grads, outs, lse, keys_values, qpos, kpos, first):
    _, local, wide = queries.shape
    _, count, length, _ = keys_values.shape
    rows = H * local
    row_spec = pl.BlockSpec((1, local, wide), lambda s: (s + first, 0, 0))
    own_spec = pl.BlockSpec((1, local, wide), lambda s: (s, 0, 0))
    return pl.pallas_call(
        flash_backward,
        grid=(count,),
        in_specs=[
            row_spec,
            row_spec,
            own_spec,
            pl.BlockSpec((1, rows, 128), lambda s: (s, 0, 0)),
            pl.BlockSpec((1, 1, length, HD), lambda s: (0, s, 0, 0)),
            pl.BlockSpec((1, 1, length, HD), lambda s: (1, s, 0, 0)),
            pl.BlockSpec((local, 128), lambda s: (0, 0)),
            pl.BlockSpec((1, length), lambda s: (0, 0)),
        ],
        out_specs=[own_spec, pl.BlockSpec((2, 1, length, HD), lambda s: (0, s, 0, 0))],
        out_shape=[
            jax.ShapeDtypeStruct((count, local, wide), f32),
            jax.ShapeDtypeStruct((2, count, length, HD), bf16),
        ],
        scratch_shapes=[pltpu.VMEM((rows, HD), f32)],
        cost_estimate=pl.CostEstimate(
            flops=10 * count * rows * length * HD,
            bytes_accessed=count * (8 * length * HD + 12 * rows * HD),
            transcendentals=count * rows * length,
        ),
        name="attend_back",
    )(queries, grads, outs, lse, keys_values, keys_values, qpos, kpos)


def shards(
    inputs,
    input_gain,
    query_weight,
    key_weight,
    value_weight,
    query_norm,
    key_norm,
    output_weight,
    attention_gain,
    feedforward_gain,
    gate_weight,
    up_weight,
    down_weight,
    closing_gain,
    cotangent,
):
    seq_count, seq_local, width = inputs.shape
    rows = seq_count * seq_local
    half = seq_count // 2
    line = lax.axis_size("r")
    rank, row, core = lax.axis_index("r"), lax.axis_index("t"), lax.axis_index("c")
    first_core, first_row = core == 0, row == 0
    chips = 4 * line
    held = input_gain.shape[0]
    held_head = query_norm.shape[0]
    q_width = H * HD

    def turn(value):
        return jnp.where(first_core, value, jnp.roll(value, half, axis=0))

    flat_in = turn(inputs).reshape(rows, width).astype(f32)
    grad_out = turn(cotangent).reshape(rows, width).astype(f32)

    position0 = (rank * 4 + row * 2 + core) * seq_local
    positions = position0 + jnp.arange(seq_local, dtype=jnp.int32)
    cos_vals, sine_vals = angles(positions, HD)

    packed = jnp.concatenate([query_weight, key_weight, value_weight], axis=1)
    half_cols = packed.shape[1] // 2
    gains = jnp.concatenate(
        [input_gain, attention_gain, feedforward_gain, closing_gain, query_norm, key_norm]
    )
    gain_row = jnp.pad(gains[None], ((0, 0), (0, half_cols - gains.shape[0])))
    mine = lax.dynamic_slice_in_dim(packed, core * half_cols, half_cols, 1)
    yours = lax.dynamic_slice_in_dim(packed, (1 - core) * half_cols, half_cols, 1)
    mine = jnp.concatenate([mine, gain_row], axis=0)
    yours = hop(jnp.concatenate([yours, gain_row], axis=0), "c")
    lower, upper = jnp.where(first_core, mine, yours), jnp.where(first_core, yours, mine)
    filled = 2 * held + 2
    padded = -(-filled // 8) * 8
    piece = jnp.concatenate(
        [
            lower[:held],
            upper[:held],
            lower[held:],
            upper[held:],
            jnp.zeros((padded - filled, half_cols), bf16),
        ],
        axis=0,
    )
    qkv_mine = gather_chips(piece)
    qkv_yours = hop(qkv_mine, "c")
    gain_table = qkv_mine[:, 2 * held : filled, : gains.shape[0]].reshape(2 * chips, -1)

    def gain_of(offset, count):
        return gain_table[:, offset : offset + count].reshape(-1).astype(f32)

    in_gain, post_gain, pre_gain, out_gain = (gain_of(i * held, held) for i in range(4))
    query_gains = gain_of(4 * held, held_head)
    key_gains = gain_of(4 * held + held_head, held_head)
    qkv_0 = jnp.where(first_core, qkv_mine, qkv_yours)[:, : 2 * held].reshape(width, half_cols)
    qkv_1 = jnp.where(first_core, qkv_yours, qkv_mine)[:, : 2 * held].reshape(width, half_cols)
    qkv_full = jnp.concatenate([qkv_0, qkv_1], axis=1)
    query_full = qkv_full[:, :q_width]
    key_full = qkv_full[:, q_width : q_width + HD]
    value_full = qkv_full[:, q_width + HD :]
    out_mine = gather_chips(output_weight)
    out_yours = hop(out_mine, "c")
    output_full = ordered(first_core, out_mine, out_yours, 1).reshape(q_width, width)

    pieces_ff = down_weight.shape[0]
    planes = 2 * line
    units = planes * pieces_ff

    def by_owner(weight):
        return weight.reshape(held, planes, 4, pieces_ff).transpose(2, 0, 1, 3).reshape(
            2, 2, held, units
        )

    both = jnp.stack([by_owner(gate_weight), by_owner(up_weight)])
    got = hop(pick(both, 1 - core, 2), "c")
    both = ordered(first_core, pick(both, core, 2), got, 2)
    got = hop(pick(both, 1 - row, 1), "t")
    both = ordered(first_row, pick(both, row, 1), got, 1).reshape(2, 4 * held, units)
    gate_full = gather_plane(both[0]).reshape(width, units)
    up_full = gather_plane(both[1]).reshape(width, units)
    down_full = gather_plane(down_weight).reshape(units, width)

    normed_in = normed(flat_in, in_gain).astype(bf16)
    qkv_raw = matmul(normed_in, qkv_full)
    query_raw = qkv_raw[:, :q_width]
    key_raw = qkv_raw[:, q_width : q_width + HD]
    value_raw = qkv_raw[:, q_width + HD :]

    def qk_forward(query_in, key_in, query_scale, key_scale):
        query_heads = normed(query_in.reshape(seq_count, seq_local, H, HD), query_scale)
        key_heads = normed(key_in.reshape(seq_count, seq_local, HD), key_scale)
        return (
            rotate(query_heads, cos_vals[:, None, :], sine_vals[:, None, :]),
            rotate(key_heads, cos_vals, sine_vals),
        )

    (query_rot, key_rot), qk_back = jax.vjp(qk_forward, query_raw, key_raw, query_gains, key_gains)
    queries = query_rot.reshape(seq_count, seq_local, q_width).astype(bf16)
    kv = jnp.stack(
        [key_rot.astype(bf16), value_raw.reshape(seq_count, seq_local, HD).astype(bf16)]
    )
    got = hop(kv[:, half:], "c")
    kv_piece = ordered(first_core, kv[:, :half], got, 2).reshape(2, half, 2 * seq_local, HD)
    near = [kv_piece] + [hop(kv_piece, "r", k) for k in range(1, line)]
    far = [hop(p, "t") for p in near]
    kv_own = jnp.concatenate(near + far, axis=2)
    kv_other = hop(kv_own, "c")
    bases = [
        (lax.rem(rank - k + line, line) * 2 + side) * (2 * seq_local)
        for side in (row, 1 - row)
        for k in range(line)
    ]
    kpos = jnp.concatenate([b + jnp.arange(2 * seq_local, dtype=jnp.int32) for b in bases])[None]
    qpos = jnp.broadcast_to(positions[:, None], (seq_local, 128))
    attn_a, lse_a = attend(queries, kv_own, qpos, kpos, 0)
    attn_b, lse_b = attend(queries, kv_other, qpos, kpos, half)
    attn_rows = jnp.concatenate([attn_a, attn_b]).reshape(rows, q_width).astype(bf16)
    attn_proj = matmul(attn_rows, output_full)
    resid = flat_in + normed(attn_proj, post_gain)

    def tokens_of_group(own):
        across = hop(own, "t")
        return jnp.concatenate([own, hop(own, "c"), across, hop(across, "c")], axis=0)

    def sum_over_group(parts):
        parts = parts.reshape(4, rows, width)
        moved = hop(parts[1::2].astype(bf16), "c").astype(f32)
        across = hop((parts[2] + moved[1]).astype(bf16), "t").astype(f32)
        return parts[0] + moved[0] + across

    normed_mid = normed(resid, pre_gain).astype(bf16)
    mids = tokens_of_group(normed_mid)
    gate_vals = matmul(mids, gate_full)
    up_vals = matmul(mids, up_full)
    hidden = gated(gate_vals, up_vals).astype(bf16)
    down_vals = sum_over_group(matmul(hidden, down_full))
    output = (resid + normed(down_vals, out_gain)).astype(bf16)

    closing_primal, closing_back = jax.vjp(normed, down_vals, out_gain)
    grad_down, grad_out_gain = closing_back(grad_out)
    grad_downs = tokens_of_group(grad_down.astype(bf16))
    down_sum = inner_rows(hidden, grad_downs).astype(bf16).reshape(planes, pieces_ff, width)
    down_weight_grad = scatter_plane(down_sum)
    grad_hidden = times_trans(grad_downs, down_full)
    gated_primal, gated_back = jax.vjp(gated, gate_vals, up_vals)
    grad_gate, grad_up = gated_back(grad_hidden)
    grad_gate_b = grad_gate.astype(bf16)
    grad_up_b = grad_up.astype(bf16)
    grad_mid = sum_over_group(
        times_trans(grad_gate_b, gate_full) + times_trans(grad_up_b, up_full)
    )

    def back_to_owner(sums):
        sums = sums.astype(bf16).reshape(2, 2, 2, held, units)
        got = hop(pick(sums, 1 - row, 1), "t")
        sums = ordered(first_row, pick(sums, row, 1), got, 1)
        got = hop(pick(sums, 1 - core, 2), "c")
        sums = ordered(first_core, pick(sums, core, 2), got, 2)
        sums = sums.reshape(2, 4, held, planes, pieces_ff).transpose(0, 2, 3, 1, 4)
        return sums.reshape(2, held, 4 * units).astype(f32)

    gate_sum = inner_rows(mids, grad_gate_b).astype(bf16).reshape(planes, 4 * held, units)
    up_sum = inner_rows(mids, grad_up_b).astype(bf16).reshape(planes, 4 * held, units)
    owned = back_to_owner(jnp.stack([scatter_plane(gate_sum), scatter_plane(up_sum)]))
    gate_weight_grad, up_weight_grad = owned[0], owned[1]

    middle_primal, middle_back = jax.vjp(normed, resid, pre_gain)
    grad_resid_part, grad_pre_gain = middle_back(grad_mid)
    grad_resid = grad_out + grad_resid_part

    post_primal, post_back = jax.vjp(normed, attn_proj, post_gain)
    grad_proj, grad_post_gain = post_back(grad_resid)
    grad_proj_b = grad_proj.astype(bf16)

    out_sum = inner_rows(attn_rows, grad_proj_b).astype(bf16)
    out_sum = out_sum.reshape(chips, 2, output_weight.shape[0], width)
    got = hop(pick(out_sum, 1 - core, 1), "c")
    out_sum = (pick(out_sum, core, 1).astype(f32) + got.astype(f32)).astype(bf16)
    output_weight_grad = scatter_chips(out_sum)

    def scatter_columns(full, extra=None):
        columns = full.shape[1] // 2
        full = full.astype(bf16)
        got = hop(lax.dynamic_slice_in_dim(full, (1 - core) * columns, columns, 1), "c")
        own = lax.dynamic_slice_in_dim(full, core * columns, columns, 1)
        own = (own.astype(f32) + got.astype(f32)).astype(bf16).reshape(chips, 2 * held, columns)
        if extra is not None:
            pad = -(-(2 * held + 2) // 8) * 8 - 2 * held - extra.shape[1]
            own = jnp.concatenate([own, extra, jnp.zeros((chips, pad, columns), bf16)], axis=1)
        sums = scatter_chips(own)
        tail = sums[2 * held :]
        sums = sums[: 2 * held].astype(bf16).reshape(2, held, columns)
        got = hop(pick(sums, 1 - core), "c")
        own = pick(sums, core)
        full = jnp.concatenate(
            [jnp.where(first_core, own, got), jnp.where(first_core, got, own)], axis=1
        )
        return full.astype(f32), tail

    grad_attn = times_trans(grad_proj_b, output_full).astype(bf16)
    grad_attn = grad_attn.reshape(seq_count, seq_local, q_width)
    dq_b, dkv_other = attend_back(queries, grad_attn, attn_b, lse_b, kv_other, qpos, kpos, half)
    dq_a, dkv_own = attend_back(queries, grad_attn, attn_a, lse_a, kv_own, qpos, kpos, 0)
    dkv = (dkv_own.astype(f32) + hop(dkv_other, "c").astype(f32)).astype(bf16)
    dkv = dkv.reshape(2, half, 2, line, 2 * seq_local, HD)
    kv_grad = None
    for k in range(line - 1, -1, -1):
        here = dkv[:, :, 0, k].astype(f32) + hop(dkv[:, :, 1, k], "t").astype(f32)
        if k > 0:
            here = hop(here.astype(bf16), "r", -k).astype(f32)
        kv_grad = here if kv_grad is None else kv_grad + here
    kv_grad = kv_grad.reshape(2, half, 2, seq_local, HD)
    got = hop(pick(kv_grad, 1 - core, 2).astype(bf16), "c").astype(f32)
    kv_grad = jnp.concatenate([pick(kv_grad, core, 2), got], axis=1)

    grad_query = jnp.concatenate([dq_a, dq_b]).reshape(seq_count, seq_local, H, HD)
    grad_query_raw, grad_key_raw, grad_query_gain, grad_key_gain = qk_back(
        (grad_query, kv_grad[0])
    )
    grad_query_b = grad_query_raw.astype(bf16)
    grad_key_b = grad_key_raw.astype(bf16)
    grad_value_b = kv_grad[1].reshape(rows, HD).astype(bf16)
    query_weight_grad, _ = scatter_columns(inner_rows(normed_in, grad_query_b))

    grad_normed_in = (
        times_trans(grad_query_b, query_full)
        + times_trans(grad_key_b, key_full)
        + times_trans(grad_value_b, value_full)
    )
    input_primal, input_back = jax.vjp(normed, flat_in, in_gain)
    grad_in_part, grad_in_gain = input_back(grad_normed_in)
    grad_inputs = (grad_resid + grad_in_part).astype(bf16)

    gain_grads = jnp.concatenate(
        [
            g.reshape(2 * chips, -1)
            for g in (
                grad_in_gain,
                grad_post_gain,
                grad_pre_gain,
                grad_out_gain,
                grad_query_gain,
                grad_key_gain,
            )
        ],
        axis=1,
    )
    count = gain_grads.shape[1]
    gain_grads = gain_grads.astype(bf16).reshape(chips, 2, count)
    gain_grads = jnp.pad(gain_grads, ((0, 0), (0, 0), (0, HD - count)))
    kv_full = jnp.concatenate(
        [inner_rows(normed_in, grad_key_b), inner_rows(normed_in, grad_value_b)], axis=1
    )
    kv_weight_grad, tail = scatter_columns(kv_full, gain_grads)
    tail = tail[:2].astype(bf16)
    gain_sum = pick(tail, core).astype(f32) + hop(pick(tail, 1 - core), "c").astype(f32)

    def gain_out(offset, size):
        return gain_sum[offset : offset + size]

    return (
        turn(output.reshape(inputs.shape)),
        turn(grad_inputs.reshape(inputs.shape)),
        gain_out(0, held),
        query_weight_grad,
        kv_weight_grad[:, :HD],
        kv_weight_grad[:, HD:],
        gain_out(4 * held, held_head),
        gain_out(4 * held + held_head, held_head),
        output_weight_grad,
        gain_out(held, held),
        gain_out(2 * held, held),
        gate_weight_grad,
        up_weight_grad,
        down_weight_grad,
        gain_out(3 * held, held),
    )


def solution(mesh):
    batch, seq = mesh.shape["batch"], mesh.shape["seq"]
    view = Mesh(mesh.devices.reshape(batch, seq // 4, 2, 2), ("batch", "r", "t", "c"))
    every = ("batch", "r", "t", "c")
    tokens = P("batch", ("r", "t", "c"), None)
    matrix, vector = P(every, None), P(every)
    return jax.shard_map(
        shards,
        mesh=view,
        in_specs=(
            tokens,
            vector,
            matrix,
            matrix,
            matrix,
            vector,
            vector,
            matrix,
            vector,
            vector,
            matrix,
            matrix,
            matrix,
            vector,
            tokens,
        ),
        out_specs=(
            tokens,
            tokens,
            vector,
            matrix,
            matrix,
            matrix,
            vector,
            vector,
            matrix,
            vector,
            vector,
            matrix,
            matrix,
            matrix,
            vector,
        ),
        check_vma=False,
    )
```
